32 devices in a mesh: groups: 2 (over x), rows: 16 (over z, y, core).
Axes of the slice: x: 2, y: 2, z: 4, core: 2. Of those that a mesh axis runs over, the one named last changes fastest.
Arguments:
- dictionary: bfloat16 [8192, 32768], P('rows'), may hold values from -0.0625 to 0.0625
- patches: bfloat16 [8192, 2048], P('rows', 'groups'), parts along dimension 1, may hold values from -6 to 6
- initial_codes: bfloat16 [32, 16, 4096], P(('groups', 'rows')), parts along dimension 0, may hold values from -3 to 3
- support: int32 [32, 16], P('groups'), parts along dimension 0, may hold values from 0 to 511, as said below
- counts: int32 [32], P('groups'), parts along dimension 0, may hold values from 4 to 16, as said below
- group_order: int32 [32], P('groups'), parts along dimension 0, may hold values from 0 to 15, each once
- penalty: float32 [32, 64], P('groups'), parts along dimension 0, may hold values from 0.05 to 0.5
Outputs:
- codes: float32 [32, 16, 4096], P(('groups', 'rows')), parts along dimension 0
The draws below stay inside these ranges and needn't reach their ends.
There are 2 independent parts, one for each index of `groups`. The reference program is written for one: setup_inputs(seed, part) draws one part's arguments, and reference() takes and returns one part's arrays. A program takes and returns all parts, laid end to end along the dimension named above; an argument that names none is the same for every part. Nothing has to cross between parts.
Inputs may be any that keep to these rules, and one draw needn't show every extreme that they name: `support`: in each group's list the first counts entries are distinct block ids; entries at positions counts and beyond are padding and are ignored. The counts of one part sum to exactly 160.
All inputs are finite; a program needn't handle non-finite values.
Results may differ from the reference program's by a relative error of at most 0.0055.
Values may be sent and summed in bfloat16 or wider, within the bound.
A program may use at most 192 MiB of HBM per device.

```python
import math
import jax
import jax.numpy as jnp
from jax import lax

PIX = 8192
NB = 512
BLOCK = 64
SLOTS = 16
PATCHES = 64
ITERS = 3
GROUPS = 16
ATOMS = 32768
BATCH = 1024
TILE = 4096


def draw_support(key, part):
    keys = jax.random.split(jax.random.fold_in(key, 11), GROUPS)
    lists = jax.vmap(lambda single: jax.random.permutation(single, NB)[:SLOTS])(keys)
    return lists.astype(jnp.int32)


def draw_counts(key, part):
    half_key, pick_key, order_key = jax.random.split(jax.random.fold_in(key, 23), 3)
    halves = GROUPS // 2
    first_half = jax.random.randint(half_key, (halves,), 4, 17)
    chosen = jax.random.randint(pick_key, (), 0, halves)
    first_half = jnp.where(jnp.arange(halves) == chosen, 16, first_half)
    joined = jnp.concatenate([first_half, 20 - first_half])
    shuffle = jax.random.permutation(order_key, GROUPS)
    return joined[shuffle].astype(jnp.int32)


def block_scale(own_key, dims, cuts, smallest, top_value):
    factor_of = 1.0
    for dim, blocks in cuts:
        steps = jax.random.uniform(jax.random.fold_in(jax.random.fold_in(own_key, 6), dim), (blocks,), jnp.float32, smallest / len(cuts), top_value / len(cuts))
        factor_of = factor_of * jnp.repeat(jnp.exp(steps), dims[dim] // blocks).reshape((-1,) + (1,) * (len(dims) - 1 - dim))
    return factor_of


def centred(stream_key, extent, deviation, most, shards=(), kind=jnp.bfloat16):
    factor_of = block_scale(stream_key, extent, shards, -0.22, 0.18) if shards else 1.0
    result = jax.random.normal(stream_key, extent, jnp.float32) * deviation * factor_of
    return jnp.minimum(jnp.maximum(result, -most), most).astype(kind)


def setup_inputs(seed: int = 0, part: int = 0) -> dict:
    seeds = jax.random.split(jax.random.key(seed), 8)
    part_keys = jax.random.split(jax.random.fold_in(seeds[7], part), 8)
    return {
        "dictionary": centred(seeds[0], (PIX, ATOMS), PIX ** -0.5, 0.0625, ((0, 16),)),
        "patches": centred(part_keys[1], (PIX, BATCH), 1.0, 6.0, ((0, 16),)),
        "initial_codes": centred(part_keys[2], (GROUPS, SLOTS, TILE), 0.5, 3.0, ((0, 16),)),
        "support": draw_support(jax.random.fold_in(jax.random.fold_in(seeds[7], part), 71), part),
        "counts": draw_counts(jax.random.fold_in(jax.random.fold_in(seeds[7], part), 71), part),
        "group_order": jax.random.permutation(part_keys[5], GROUPS).astype(jnp.int32),
        "penalty": jnp.clip(jnp.exp(jax.random.uniform(part_keys[6], (GROUPS, PATCHES), jnp.float32, math.log(0.05), math.log(0.5))), 0.05, 0.5),
    }


def momentum_list():
    values = []
    tvalue = 1.0
    for turn in range(ITERS):
        tnext = (1.0 + (1.0 + 4.0 * tvalue * tvalue) ** 0.5) / 2.0
        values.append((tvalue - 1.0) / tnext)
        tvalue = tnext
    return values


def reference(dictionary, patches, initial_codes, support, counts, group_order, penalty):
    blocks_all = dictionary.reshape(PIX, NB, BLOCK)
    momenta = momentum_list()

    def one_group(position):
        group = group_order[position]
        block_ids = support[group]
        dict_blocks = jnp.take(blocks_all, block_ids, axis=1).astype(jnp.float32)
        target = lax.dynamic_slice_in_dim(patches, (group * PATCHES).astype(jnp.int32), PATCHES, 1).astype(jnp.float32)
        live_mask = (jnp.arange(SLOTS) < counts[group]).astype(jnp.float32)[:, None, None]
        thresh = (0.5 * penalty[group])[None, :, None]
        previous = initial_codes[position].reshape(SLOTS, PATCHES, BLOCK).astype(jnp.float32) * live_mask
        point = previous
        for weight in momenta:
            rounded = lax.optimization_barrier(point.astype(jnp.bfloat16)).astype(jnp.float32)
            residual = jnp.einsum("psa,sna->pn", dict_blocks, rounded, precision=lax.Precision.HIGHEST) - target
            residual = lax.optimization_barrier(residual.astype(jnp.bfloat16)).astype(jnp.float32)
            gradient = jnp.einsum("pn,psa->sna", residual, dict_blocks, precision=lax.Precision.HIGHEST)
            stepped = point - 0.5 * gradient
            current = (stepped - jnp.clip(stepped, -thresh, thresh)) * live_mask
            point = current + weight * (current - previous)
            previous = current
        return previous.reshape(SLOTS, PATCHES * BLOCK)

    return lax.map(one_group, jnp.arange(GROUPS, dtype=jnp.int32))
```

```python
import functools

import jax
import jax.numpy as jnp
from jax import lax
from jax.experimental import pallas as pl
from jax.experimental.pallas import tpu as pltpu
from jax.sharding import PartitionSpec as P

BLOCK = 64
SLOTS = 16
PATCHES = 64
ITERS = 3
LIVE = 10
PER_STEP = 8
F32 = jnp.float32
BF16 = jnp.bfloat16
VMEM = pltpu.VMEM


def momentum_list():
    values = []
    tvalue = 1.0
    for turn in range(ITERS):
        tnext = (1.0 + (1.0 + 4.0 * tvalue * tvalue) ** 0.5) / 2.0
        values.append((tvalue - 1.0) / tnext)
        tvalue = tnext
    return values


def gather_kernel(ids_ref, *refs):
    out_ref = refs[-1]
    step = pl.program_id(0)
    lane = lax.broadcasted_iota(jnp.int32, (out_ref.shape[1], 128), 1)
    for pair in range(PER_STEP // 2):
        sides = []
        for side in range(2):
            slot = 2 * pair + side
            half = ids_ref[step * PER_STEP + slot] % 2
            tile = refs[slot][...].astype(F32)
            turned = pltpu.roll(tile, 64, 1)
            sides.append(jnp.where(half == side, tile, turned))
        both = jnp.where(lane < 64, sides[0], sides[1]).astype(BF16)
        out_ref[pair // 2, :, pl.ds((pair % 2) * 128, 128)] = both


def gather_blocks(dictionary, ids):
    rows = dictionary.shape[0]
    entries = ids.shape[0]

    def spec(slot):
        return pl.BlockSpec((rows, 128), lambda i, ids_ref: (0, ids_ref[i * PER_STEP + slot] // 2))

    return pl.pallas_call(
        gather_kernel,
        out_shape=jax.ShapeDtypeStruct((entries // 4, rows, 256), BF16),
        grid_spec=pltpu.PrefetchScalarGridSpec(
            num_scalar_prefetch=1,
            grid=(entries // PER_STEP,),
            in_specs=[spec(slot) for slot in range(PER_STEP)],
            out_specs=pl.BlockSpec((PER_STEP // 4, rows, 256), lambda i, ids_ref: (i, 0, 0)),
        ),
        name="gather_blocks",
    )(ids, *([dictionary] * PER_STEP))


def share_kernel(first_ref, last_ref, split_ref, s_ref, z_ref, y_ref, out_ref, r_ref, rb_ref):
    quads = s_ref.shape[0]
    lane = lax.broadcasted_iota(jnp.int32, (PATCHES, 256), 1) // BLOCK
    r_ref[...] = -y_ref[...].astype(F32)

    def forward(quad, carry):
        z = jnp.concatenate([z_ref[2 * quad], z_ref[2 * quad + 1]], axis=1).astype(F32)
        mask = lane < split_ref[quad]
        zz = jnp.concatenate([jnp.where(mask, z, 0.0), jnp.where(mask, 0.0, z)], axis=0).astype(BF16)
        term = lax.dot_general(zz, s_ref[quad], (((1,), (1,)), ((), ())), preferred_element_type=F32)
        r_ref[first_ref[quad]] += term[:PATCHES]
        r_ref[last_ref[quad]] += term[PATCHES:]
        return carry

    lax.fori_loop(0, quads, forward, 0, unroll=2)
    rb_ref[...] = r_ref[...].astype(BF16)

    def backward(quad, carry):
        rr = jnp.concatenate([rb_ref[first_ref[quad]], rb_ref[last_ref[quad]]], axis=0)
        gr = jnp.dot(rr, s_ref[quad], preferred_element_type=F32)
        g = jnp.where(lane < split_ref[quad], gr[:PATCHES], gr[PATCHES:]).astype(BF16)
        out_ref[2 * quad] = g[:, :128]
        out_ref[2 * quad + 1] = g[:, 128:]
        return carry

    lax.fori_loop(0, quads, backward, 0, unroll=2)


def gradient_share(first, last, split, blocks, z, targets):
    groups, patches, rows = targets.shape
    smem = pl.BlockSpec(memory_space=pltpu.SMEM)
    vmem = pl.BlockSpec(memory_space=VMEM)
    return pl.pallas_call(
        share_kernel,
        out_shape=jax.ShapeDtypeStruct(z.shape, BF16),
        in_specs=[smem, smem, smem, vmem, vmem, vmem],
        out_specs=vmem,
        scratch_shapes=[VMEM((groups, patches, rows), F32), VMEM((groups, patches, rows), BF16)],
        compiler_params=pltpu.CompilerParams(vmem_limit_bytes=40 * 1024 * 1024),
        name="gradient_share",
    )(first, last, split, blocks, z, targets)


class Place:
    def __init__(self, devices):
        self.me = lax.axis_index("rows")
        self.fars = devices // 4
        self.core = self.me % 2
        self.near = (self.me // 2) % 2
        self.far = self.me // 4

    def index(self, far, near, core):
        return (far * 2 + near) * 2 + core

    def far_at(self, distance):
        return (self.far + distance) % self.fars

    def far_before(self, distance):
        return (self.far + self.fars - distance) % self.fars

    def far_peer(self, distance):
        return self.index(self.far_at(distance), self.near, self.core)

    def near_peer(self):
        return self.index(self.far, 1 - self.near, self.core)

    def core_peer(self):
        return self.index(self.far, self.near, 1 - self.core)


def send(src, dst, send_sem, recv_sem, peer):
    copy = pltpu.make_async_remote_copy(
        src_ref=src,
        dst_ref=dst,
        send_sem=send_sem,
        recv_sem=recv_sem,
        device_id=(lax.axis_index("groups"), peer),
        device_id_type=pl.DeviceIdType.MESH,
    )
    copy.start()
    return copy


def greet(at):
    barrier = pltpu.get_barrier_semaphore()
    peers = [at.core_peer(), at.near_peer()] + [at.far_peer(d) for d in range(1, at.fars)]
    for peer in peers:
        pl.semaphore_signal(
            barrier, inc=1, device_id=(lax.axis_index("groups"), peer), device_id_type=pl.DeviceIdType.MESH
        )
    pl.semaphore_wait(barrier, len(peers))


def spread(at, all_ref, sems):
    far_s, far_r, near_s, near_r, core_s, core_r = sems
    mine = all_ref.at[at.me]
    far_copies = [
        send(mine, mine, far_s.at[d - 1], far_r.at[d - 1], at.far_peer(d)) for d in range(1, at.fars)
    ]
    near_copies = [send(mine, mine, near_s.at[0], near_r.at[0], at.near_peer())]
    core_copies = [send(mine, mine, core_s.at[0], core_r.at[0], at.core_peer())]
    slot = 1
    for d in range(at.fars):
        if d:
            far_copies[d - 1].wait_recv()
            came = all_ref.at[at.index(at.far_before(d), at.near, at.core)]
            near_copies.append(send(came, came, near_s.at[d], near_r.at[d], at.near_peer()))
            core_copies.append(send(came, came, core_s.at[slot], core_r.at[slot], at.core_peer()))
            slot += 1
        if d:
            near_copies[d - 1].wait_recv()
            came = all_ref.at[at.index(at.far_before(d - 1), 1 - at.near, at.core)]
            core_copies.append(send(came, came, core_s.at[slot], core_r.at[slot], at.core_peer()))
            slot += 1
    last = at.fars - 1
    near_copies[last].wait_recv()
    came = all_ref.at[at.index(at.far_before(last), 1 - at.near, at.core)]
    core_copies.append(send(came, came, core_s.at[slot], core_r.at[slot], at.core_peer()))
    for copy in core_copies:
        copy.wait_recv()
    for copy in far_copies + near_copies + core_copies:
        copy.wait_send()


def gather_codes_kernel(devices, mine_ref, all_ref, own_sem, *sems):
    at = Place(devices)
    own = pltpu.make_async_copy(mine_ref, all_ref.at[at.me], own_sem)
    own.start()
    greet(at)
    own.wait()
    spread(at, all_ref, sems)


def spread_sems(devices):
    fars = devices // 4
    dma = pltpu.SemaphoreType.DMA
    return [dma((fars - 1,)), dma((fars - 1,)), dma((fars,)), dma((fars,)), dma((2 * fars,)), dma((2 * fars,))]


def gather_codes(devices, mine):
    vmem = pl.BlockSpec(memory_space=VMEM)
    return pl.pallas_call(
        functools.partial(gather_codes_kernel, devices),
        out_shape=jax.ShapeDtypeStruct((devices,) + mine.shape, BF16),
        in_specs=[vmem],
        out_specs=vmem,
        scratch_shapes=[pltpu.SemaphoreType.DMA] + spread_sems(devices),
        compiler_params=pltpu.CompilerParams(collective_id=0, has_side_effects=True),
        name="gather_codes",
    )(mine)


def step_kernel(
    devices, weight, share_ref, point_ref, prev_ref, thr_ref, all_ref, newpoint_ref, newprev_ref,
    got_core, got_near, got_far, sum_core, sum_near, kept,
    c_s, c_r, n_s, n_r, f_s, f_r, *sems,
):
    at = Place(devices)
    fars = at.fars
    greet(at)
    order = list(range(1, fars)) + [0]
    core_copies = {}
    for flip in (1, 0):
        for d in order:
            near = at.near if flip == 0 else 1 - at.near
            chunk = share_ref.at[at.index(at.far_at(d), near, 1 - at.core)]
            slot = flip * fars + d
            core_copies[flip, d] = send(chunk, got_core.at[slot], c_s.at[slot], c_r.at[slot], at.core_peer())
    near_copies = {}
    for d in order:
        core_copies[1, d].wait_recv()
        own = share_ref[at.index(at.far_at(d), 1 - at.near, at.core)].astype(F32)
        sum_core[d] = (own + got_core[fars + d].astype(F32)).astype(BF16)
        near_copies[d] = send(sum_core.at[d], got_near.at[d], n_s.at[d], n_r.at[d], at.near_peer())
    far_copies = {}
    for d in order:
        core_copies[0, d].wait_recv()
        own = share_ref[at.index(at.far_at(d), at.near, at.core)].astype(F32)
        total = own + got_core[d].astype(F32)
        near_copies[d].wait_recv()
        total = total + got_near[d].astype(F32)
        if d:
            sum_near[d - 1] = total.astype(BF16)
            far_copies[d] = send(sum_near.at[d - 1], got_far.at[d - 1], f_s.at[d - 1], f_r.at[d - 1], at.far_peer(d))
        else:
            kept[...] = total
    for d in range(1, fars):
        far_copies[d].wait_recv()
        kept[...] += got_far[d - 1].astype(F32)
    stepped = point_ref[...] - 0.5 * kept[...]
    thr = thr_ref[...]
    current = stepped - jnp.clip(stepped, -thr, thr)
    newprev_ref[...] = current
    point = current if weight is None else current + weight * (current - prev_ref[...])
    newpoint_ref[...] = point
    all_ref[at.me] = point.astype(BF16)
    for copy in list(core_copies.values()) + list(near_copies.values()) + list(far_copies.values()):
        copy.wait_send()
    spread(at, all_ref, sems)


def code_step(devices, turn, weight, share, point, prev, thr):
    fars = devices // 4
    chunk = point.shape
    dma = pltpu.SemaphoreType.DMA
    vmem = pl.BlockSpec(memory_space=VMEM)
    return pl.pallas_call(
        functools.partial(step_kernel, devices, weight),
        out_shape=(
            jax.ShapeDtypeStruct(share.shape, BF16),
            jax.ShapeDtypeStruct(chunk, F32),
            jax.ShapeDtypeStruct(chunk, F32),
        ),
        in_specs=[vmem] * 4,
        out_specs=(vmem, vmem, vmem),
        scratch_shapes=[
            VMEM((2 * fars,) + chunk, BF16),
            VMEM((fars,) + chunk, BF16),
            VMEM((fars - 1,) + chunk, BF16),
            VMEM((fars,) + chunk, BF16),
            VMEM((fars - 1,) + chunk, BF16),
            VMEM(chunk, F32),
            dma((2 * fars,)), dma((2 * fars,)), dma((fars,)), dma((fars,)), dma((fars - 1,)), dma((fars - 1,)),
        ]
        + spread_sems(devices),
        compiler_params=pltpu.CompilerParams(
            collective_id=1 + turn, has_side_effects=True, vmem_limit_bytes=40 * 1024 * 1024
        ),
        name="code_step%d" % turn,
    )(share, point, prev, thr)


def local(dictionary, patches, initial_codes, support, counts, group_order, penalty):
    rows = dictionary.shape[0]
    groups = group_order.shape[0]
    devices = lax.axis_size("rows")
    me = lax.axis_index("rows")
    entries = LIVE * groups
    pairs = entries // 2
    chunk_pairs = pairs // devices
    chunk_rows = chunk_pairs * PATCHES

    mine = initial_codes.reshape(SLOTS // 2, 2, PATCHES, BLOCK).transpose(0, 2, 1, 3)
    mine = mine.reshape(SLOTS // 2 * PATCHES, 2 * BLOCK)
    start_all = gather_codes(devices, mine).reshape(groups * SLOTS // 2, PATCHES, 2 * BLOCK)

    ends = jnp.cumsum(counts)
    starts = ends - counts
    entry = jnp.arange(entries, dtype=jnp.int32)
    group_of = jnp.sum((entry[:, None] >= ends[None, :]).astype(jnp.int32), axis=1)
    slot_of = entry - jnp.take(starts, group_of)
    ids = jnp.take(support.reshape(-1), group_of * SLOTS + slot_of)
    quads = group_of.reshape(-1, 4)
    first, last = quads[:, 0], quads[:, 3]
    split = jnp.sum((quads == first[:, None]).astype(jnp.int32), axis=1)
    seat = jnp.argmax(group_order[None, :] == group_of[:, None], axis=1).astype(jnp.int32)

    blocks = gather_blocks(dictionary, ids)
    targets = patches.T.reshape(groups, PATCHES, rows)

    source = (seat * (SLOTS // 2) + slot_of // 2).reshape(pairs, 2)
    half = (slot_of % 2).reshape(pairs, 2)[:, :, None, None] == 0

    def side(which):
        both = jnp.take(start_all, source[:, which], axis=0)
        return jnp.where(half[:, which], both[..., :BLOCK], both[..., BLOCK:])

    z_all = jnp.concatenate([side(0), side(1)], axis=2)
    thr_all = 0.5 * jnp.take(penalty, group_of, axis=0)
    own_thr = lax.dynamic_slice_in_dim(thr_all.reshape(pairs, 2, PATCHES), me * chunk_pairs, chunk_pairs, 0)
    thr = jnp.repeat(own_thr.transpose(0, 2, 1).reshape(chunk_rows, 2), BLOCK, axis=1)
    point = lax.dynamic_slice_in_dim(z_all, me * chunk_pairs, chunk_pairs, 0)
    point = point.reshape(chunk_rows, 2 * BLOCK).astype(F32)
    prev = point
    momenta = momentum_list()
    for turn in range(ITERS):
        share = gradient_share(first, last, split, blocks, z_all, targets)
        weight = momenta[turn] if turn + 1 < ITERS else None
        share = share.reshape(devices, chunk_rows, 2 * BLOCK)
        z_all, point, prev = code_step(devices, turn, weight, share, point, prev, thr)
        z_all = z_all.reshape(pairs, PATCHES, 2 * BLOCK)

    group = lax.dynamic_index_in_dim(group_order, me, 0, keepdims=False)
    begin = jnp.take(starts, group)
    live = jnp.take(counts, group)
    wanted = begin // 2 + jnp.arange(SLOTS // 2 + 1, dtype=jnp.int32)
    near = jnp.take(z_all, jnp.minimum(wanted, pairs - 1), axis=0).astype(F32)
    near = near.reshape(SLOTS // 2 + 1, PATCHES, 2, BLOCK).transpose(0, 2, 1, 3)
    near = near.reshape(SLOTS + 2, PATCHES, BLOCK)
    codes = lax.dynamic_slice_in_dim(near, begin % 2, SLOTS, 0)
    codes = jnp.where((jnp.arange(SLOTS) < live)[:, None, None], codes, 0.0)
    return codes.reshape(1, SLOTS, PATCHES * BLOCK)


def solution(mesh):
    in_specs = (
        P("rows", None),
        P("rows", "groups"),
        P(("groups", "rows"), None, None),
        P("groups", None),
        P("groups"),
        P("groups"),
        P("groups", None),
    )
    out_specs = P(("groups", "rows"), None, None)
    return jax.shard_map(local, mesh=mesh, in_specs=in_specs, out_specs=out_specs, check_vma=False)
```

```python
import functools

import jax
import jax.numpy as jnp
from jax import lax
from jax.experimental import pallas as pl
from jax.experimental.pallas import tpu as pltpu
from jax.sharding import PartitionSpec as P

BLOCK = 64
SLOTS = 16
PATCHES = 64
ITERS = 3
LIVE = 10
PER_STEP = 8
F32 = jnp.float32
BF16 = jnp.bfloat16
VMEM = pltpu.VMEM


def momentum_list():
    values = []
    tvalue = 1.0
    for turn in range(ITERS):
        tnext = (1.0 + (1.0 + 4.0 * tvalue * tvalue) ** 0.5) / 2.0
        values.append((tvalue - 1.0) / tnext)
        tvalue = tnext
    return values


def gather_kernel(ids_ref, *refs):
    out_ref = refs[-1]
    step = pl.program_id(0)
    for pair in range(PER_STEP // 2):
        for side in range(2):
            slot = 2 * pair + side
            tile_ref = refs[slot]
            where_to = pl.ds((pair % 2) * 128 + side * 64, 64)
            half = ids_ref[step * PER_STEP + slot] % 2

            @pl.when(half == 0)
            def _(tile_ref=tile_ref, where_to=where_to, pair=pair):
                out_ref[pair // 2, :, where_to] = tile_ref[:, :64]

            @pl.when(half == 1)
            def _(tile_ref=tile_ref, where_to=where_to, pair=pair):
                out_ref[pair // 2, :, where_to] = tile_ref[:, 64:]


def gather_blocks(dictionary, ids):
    rows = dictionary.shape[0]
    entries = ids.shape[0]

    def spec(slot):
        return pl.BlockSpec((rows, 128), lambda i, ids_ref: (0, ids_ref[i * PER_STEP + slot] // 2))

    return pl.pallas_call(
        gather_kernel,
        out_shape=jax.ShapeDtypeStruct((entries // 4, rows, 256), BF16),
        grid_spec=pltpu.PrefetchScalarGridSpec(
            num_scalar_prefetch=1,
            grid=(entries // PER_STEP,),
            in_specs=[spec(slot) for slot in range(PER_STEP)],
            out_specs=pl.BlockSpec((PER_STEP // 4, rows, 256), lambda i, ids_ref: (i, 0, 0)),
        ),
        name="gather_blocks",
    )(ids, *([dictionary] * PER_STEP))


def share_kernel(first_ref, last_ref, split_ref, s_ref, z_ref, y_ref, out_ref, r_ref, rb_ref):
    quads = s_ref.shape[0]
    lane = lax.broadcasted_iota(jnp.int32, (PATCHES, 256), 1) // BLOCK
    r_ref[...] = -y_ref[...].astype(F32)

    def forward(quad, carry):
        z = jnp.concatenate([z_ref[2 * quad], z_ref[2 * quad + 1]], axis=1).astype(F32)
        mask = lane < split_ref[quad]
        zz = jnp.concatenate([jnp.where(mask, z, 0.0), jnp.where(mask, 0.0, z)], axis=0).astype(BF16)
        term = lax.dot_general(zz, s_ref[quad], (((1,), (1,)), ((), ())), preferred_element_type=F32)
        r_ref[first_ref[quad]] += term[:PATCHES]
        r_ref[last_ref[quad]] += term[PATCHES:]
        return carry

    lax.fori_loop(0, quads, forward, 0, unroll=4)
    rb_ref[...] = r_ref[...].astype(BF16)

    def backward(quad, carry):
        rr = jnp.concatenate([rb_ref[first_ref[quad]], rb_ref[last_ref[quad]]], axis=0)
        gr = jnp.dot(rr, s_ref[quad], preferred_element_type=F32)
        g = jnp.where(lane < split_ref[quad], gr[:PATCHES], gr[PATCHES:]).astype(BF16)
        out_ref[2 * quad] = g[:, :128]
        out_ref[2 * quad + 1] = g[:, 128:]
        return carry

    lax.fori_loop(0, quads, backward, 0, unroll=4)


def gradient_share(first, last, split, blocks, z, targets):
    groups, patches, rows = targets.shape
    smem = pl.BlockSpec(memory_space=pltpu.SMEM)
    vmem = pl.BlockSpec(memory_space=VMEM)
    return pl.pallas_call(
        share_kernel,
        out_shape=jax.ShapeDtypeStruct(z.shape, BF16),
        in_specs=[smem, smem, smem, vmem, vmem, vmem],
        out_specs=vmem,
        scratch_shapes=[VMEM((groups, patches, rows), F32), VMEM((groups, patches, rows), BF16)],
        compiler_params=pltpu.CompilerParams(vmem_limit_bytes=40 * 1024 * 1024),
        name="gradient_share",
    )(first, last, split, blocks, z, targets)


class Place:
    def __init__(self, devices):
        self.me = lax.axis_index("rows")
        self.fars = devices // 4
        self.core = self.me % 2
        self.near = (self.me // 2) % 2
        self.far = self.me // 4

    def index(self, far, near, core):
        return (far * 2 + near) * 2 + core

    def far_at(self, distance):
        return (self.far + distance) % self.fars

    def far_before(self, distance):
        return (self.far + self.fars - distance) % self.fars

    def far_peer(self, distance):
        return self.index(self.far_at(distance), self.near, self.core)

    def near_peer(self):
        return self.index(self.far, 1 - self.near, self.core)

    def core_peer(self):
        return self.index(self.far, self.near, 1 - self.core)


def send(src, dst, send_sem, recv_sem, peer):
    copy = pltpu.make_async_remote_copy(
        src_ref=src,
        dst_ref=dst,
        send_sem=send_sem,
        recv_sem=recv_sem,
        device_id=(lax.axis_index("groups"), peer),
        device_id_type=pl.DeviceIdType.MESH,
    )
    copy.start()
    return copy


def greet(at):
    barrier = pltpu.get_barrier_semaphore()
    peers = [at.core_peer(), at.near_peer()] + [at.far_peer(d) for d in range(1, at.fars)]
    for peer in peers:
        pl.semaphore_signal(
            barrier, inc=1, device_id=(lax.axis_index("groups"), peer), device_id_type=pl.DeviceIdType.MESH
        )
    pl.semaphore_wait(barrier, len(peers))


def spread(at, all_ref, sems):
    far_s, far_r, near_s, near_r, core_s, core_r = sems
    mine = all_ref.at[at.me]
    far_copies = [
        send(mine, mine, far_s.at[d - 1], far_r.at[d - 1], at.far_peer(d)) for d in range(1, at.fars)
    ]
    near_copies = [send(mine, mine, near_s.at[0], near_r.at[0], at.near_peer())]
    core_copies = [send(mine, mine, core_s.at[0], core_r.at[0], at.core_peer())]
    slot = 1
    for d in range(at.fars):
        if d:
            far_copies[d - 1].wait_recv()
            came = all_ref.at[at.index(at.far_before(d), at.near, at.core)]
            near_copies.append(send(came, came, near_s.at[d], near_r.at[d], at.near_peer()))
            core_copies.append(send(came, came, core_s.at[slot], core_r.at[slot], at.core_peer()))
            slot += 1
        if d:
            near_copies[d - 1].wait_recv()
            came = all_ref.at[at.index(at.far_before(d - 1), 1 - at.near, at.core)]
            core_copies.append(send(came, came, core_s.at[slot], core_r.at[slot], at.core_peer()))
            slot += 1
    last = at.fars - 1
    near_copies[last].wait_recv()
    came = all_ref.at[at.index(at.far_before(last), 1 - at.near, at.core)]
    core_copies.append(send(came, came, core_s.at[slot], core_r.at[slot], at.core_peer()))
    for copy in core_copies:
        copy.wait_recv()
    for copy in far_copies + near_copies + core_copies:
        copy.wait_send()


def gather_codes_kernel(devices, mine_ref, all_ref, own_sem, *sems):
    at = Place(devices)
    own = pltpu.make_async_copy(mine_ref, all_ref.at[at.me], own_sem)
    own.start()
    greet(at)
    own.wait()
    spread(at, all_ref, sems)


def spread_sems(devices):
    fars = devices // 4
    dma = pltpu.SemaphoreType.DMA
    return [dma((fars - 1,)), dma((fars - 1,)), dma((fars,)), dma((fars,)), dma((2 * fars,)), dma((2 * fars,))]


def gather_codes(devices, mine):
    vmem = pl.BlockSpec(memory_space=VMEM)
    return pl.pallas_call(
        functools.partial(gather_codes_kernel, devices),
        out_shape=jax.ShapeDtypeStruct((devices,) + mine.shape, BF16),
        in_specs=[vmem],
        out_specs=vmem,
        scratch_shapes=[pltpu.SemaphoreType.DMA] + spread_sems(devices),
        compiler_params=pltpu.CompilerParams(collective_id=0, has_side_effects=True),
        name="gather_codes",
    )(mine)


def step_kernel(
    devices, weight, share_ref, point_ref, prev_ref, thr_ref, all_ref, newpoint_ref, newprev_ref,
    got_core, got_near, got_far, sum_core, sum_near, kept,
    c_s, c_r, n_s, n_r, f_s, f_r, *sems,
):
    at = Place(devices)
    fars = at.fars
    greet(at)
    order = list(range(1, fars)) + [0]
    core_copies = {}
    for flip in (1, 0):
        for d in order:
            near = at.near if flip == 0 else 1 - at.near
            chunk = share_ref.at[at.index(at.far_at(d), near, 1 - at.core)]
            slot = flip * fars + d
            core_copies[flip, d] = send(chunk, got_core.at[slot], c_s.at[slot], c_r.at[slot], at.core_peer())
    near_copies = {}
    for d in order:
        core_copies[1, d].wait_recv()
        own = share_ref[at.index(at.far_at(d), 1 - at.near, at.core)].astype(F32)
        sum_core[d] = (own + got_core[fars + d].astype(F32)).astype(BF16)
        near_copies[d] = send(sum_core.at[d], got_near.at[d], n_s.at[d], n_r.at[d], at.near_peer())
    far_copies = {}
    for d in order:
        core_copies[0, d].wait_recv()
        own = share_ref[at.index(at.far_at(d), at.near, at.core)].astype(F32)
        total = own + got_core[d].astype(F32)
        near_copies[d].wait_recv()
        total = total + got_near[d].astype(F32)
        if d:
            sum_near[d - 1] = total.astype(BF16)
            far_copies[d] = send(sum_near.at[d - 1], got_far.at[d - 1], f_s.at[d - 1], f_r.at[d - 1], at.far_peer(d))
        else:
            kept[...] = total
    for d in range(1, fars):
        far_copies[d].wait_recv()
        kept[...] += got_far[d - 1].astype(F32)
    stepped = point_ref[...] - 0.5 * kept[...]
    thr = thr_ref[...]
    current = stepped - jnp.clip(stepped, -thr, thr)
    newprev_ref[...] = current
    point = current if weight is None else current + weight * (current - prev_ref[...])
    newpoint_ref[...] = point
    all_ref[at.me] = point.astype(BF16)
    for copy in list(core_copies.values()) + list(near_copies.values()) + list(far_copies.values()):
        copy.wait_send()
    spread(at, all_ref, sems)


def code_step(devices, turn, weight, share, point, prev, thr):
    fars = devices // 4
    chunk = point.shape
    dma = pltpu.SemaphoreType.DMA
    vmem = pl.BlockSpec(memory_space=VMEM)
    return pl.pallas_call(
        functools.partial(step_kernel, devices, weight),
        out_shape=(
            jax.ShapeDtypeStruct(share.shape, BF16),
            jax.ShapeDtypeStruct(chunk, F32),
            jax.ShapeDtypeStruct(chunk, F32),
        ),
        in_specs=[vmem] * 4,
        out_specs=(vmem, vmem, vmem),
        scratch_shapes=[
            VMEM((2 * fars,) + chunk, BF16),
            VMEM((fars,) + chunk, BF16),
            VMEM((fars - 1,) + chunk, BF16),
            VMEM((fars,) + chunk, BF16),
            VMEM((fars - 1,) + chunk, BF16),
            VMEM(chunk, F32),
            dma((2 * fars,)), dma((2 * fars,)), dma((fars,)), dma((fars,)), dma((fars - 1,)), dma((fars - 1,)),
        ]
        + spread_sems(devices),
        compiler_params=pltpu.CompilerParams(
            collective_id=1 + turn, has_side_effects=True, vmem_limit_bytes=40 * 1024 * 1024
        ),
        name="code_step%d" % turn,
    )(share, point, prev, thr)


def local(dictionary, patches, initial_codes, support, counts, group_order, penalty):
    rows = dictionary.shape[0]
    groups = group_order.shape[0]
    devices = lax.axis_size("rows")
    me = lax.axis_index("rows")
    entries = LIVE * groups
    pairs = entries // 2
    chunk_pairs = pairs // devices
    chunk_rows = chunk_pairs * PATCHES

    mine = initial_codes.reshape(SLOTS // 2, 2, PATCHES, BLOCK).transpose(0, 2, 1, 3)
    mine = mine.reshape(SLOTS // 2 * PATCHES, 2 * BLOCK)
    start_all = lax.all_gather(mine, "rows", axis=0).reshape(groups * SLOTS // 2, PATCHES, 2 * BLOCK)

    ends = jnp.cumsum(counts)
    starts = ends - counts
    entry = jnp.arange(entries, dtype=jnp.int32)
    group_of = jnp.sum((entry[:, None] >= ends[None, :]).astype(jnp.int32), axis=1)
    slot_of = entry - jnp.max(jnp.where(entry[:, None] >= starts[None, :], starts[None, :], 0), axis=1)
    ids = jnp.take(support.reshape(-1), group_of * SLOTS + slot_of)
    quads = group_of.reshape(-1, 4)
    first, last = quads[:, 0], quads[:, 3]
    split = jnp.sum((quads == first[:, None]).astype(jnp.int32), axis=1)
    seats = jnp.arange(groups, dtype=jnp.int32)[None, :]
    seat = jnp.sum(jnp.where(group_order[None, :] == group_of[:, None], seats, 0), axis=1)

    blocks = gather_blocks(dictionary, ids)
    targets = patches.T.reshape(groups, PATCHES, rows)

    source = (seat * (SLOTS // 2) + slot_of // 2).reshape(pairs, 2)
    half = (slot_of % 2).reshape(pairs, 2)[:, :, None, None] == 0

    def side(which):
        both = jnp.take(start_all, source[:, which], axis=0)
        return jnp.where(half[:, which], both[..., :BLOCK], both[..., BLOCK:])

    z_all = jnp.concatenate([side(0), side(1)], axis=2)
    thr_all = 0.5 * jnp.take(penalty, group_of, axis=0)
    own_thr = lax.dynamic_slice_in_dim(thr_all.reshape(pairs, 2, PATCHES), me * chunk_pairs, chunk_pairs, 0)
    thr = jnp.repeat(own_thr.transpose(0, 2, 1).reshape(chunk_rows, 2), BLOCK, axis=1)
    point = lax.dynamic_slice_in_dim(z_all, me * chunk_pairs, chunk_pairs, 0)
    point = point.reshape(chunk_rows, 2 * BLOCK).astype(F32)
    prev = point
    momenta = momentum_list()
    for turn in range(ITERS):
        share = gradient_share(first, last, split, blocks, z_all, targets)
        weight = momenta[turn] if turn + 1 < ITERS else None
        share = share.reshape(devices, chunk_rows, 2 * BLOCK)
        z_all, point, prev = code_step(devices, turn, weight, share, point, prev, thr)
        z_all = z_all.reshape(pairs, PATCHES, 2 * BLOCK)

    group = lax.dynamic_index_in_dim(group_order, me, 0, keepdims=False)
    begin = jnp.take(starts, group)
    live = jnp.take(counts, group)
    wanted = begin // 2 + jnp.arange(SLOTS // 2 + 1, dtype=jnp.int32)
    near = jnp.take(z_all, jnp.minimum(wanted, pairs - 1), axis=0).astype(F32)
    near = near.reshape(SLOTS // 2 + 1, PATCHES, 2, BLOCK).transpose(0, 2, 1, 3)
    near = near.reshape(SLOTS + 2, PATCHES, BLOCK)
    codes = lax.dynamic_slice_in_dim(near, begin % 2, SLOTS, 0)
    codes = jnp.where((jnp.arange(SLOTS) < live)[:, None, None], codes, 0.0)
    return codes.reshape(1, SLOTS, PATCHES * BLOCK)


def solution(mesh):
    in_specs = (
        P("rows", None),
        P("rows", "groups"),
        P(("groups", "rows"), None, None),
        P("groups", None),
        P("groups"),
        P("groups"),
        P("groups", None),
    )
    out_specs = P(("groups", "rows"), None, None)
    return jax.shard_map(local, mesh=mesh, in_specs=in_specs, out_specs=out_specs, check_vma=False)
```

```python
import functools

import jax
import jax.numpy as jnp
from jax import lax
from jax.experimental import pallas as pl
from jax.experimental.pallas import tpu as pltpu
from jax.sharding import PartitionSpec as P

BLOCK = 64
SLOTS = 16
PATCHES = 64
ITERS = 3
LIVE = 10
PER_STEP = 16
F32 = jnp.float32
BF16 = jnp.bfloat16
VMEM = pltpu.VMEM


def momentum_list():
    values = []
    tvalue = 1.0
    for turn in range(ITERS):
        tnext = (1.0 + (1.0 + 4.0 * tvalue * tvalue) ** 0.5) / 2.0
        values.append((tvalue - 1.0) / tnext)
        tvalue = tnext
    return values


def gather_kernel(ids_ref, *refs):
    out_ref = refs[-1]
    step = pl.program_id(0)
    for pair in range(PER_STEP // 2):
        for side in range(2):
            slot = 2 * pair + side
            tile_ref = refs[slot]
            where_to = pl.ds((pair % 2) * 128 + side * 64, 64)
            half = ids_ref[step * PER_STEP + slot] % 2

            @pl.when(half == 0)
            def _(tile_ref=tile_ref, where_to=where_to, pair=pair):
                out_ref[pair // 2, :, where_to] = tile_ref[:, :64]

            @pl.when(half == 1)
            def _(tile_ref=tile_ref, where_to=where_to, pair=pair):
                out_ref[pair // 2, :, where_to] = tile_ref[:, 64:]


def gather_blocks(dictionary, ids):
    rows = dictionary.shape[0]
    entries = ids.shape[0]

    def spec(slot):
        return pl.BlockSpec((rows, 128), lambda i, ids_ref: (0, ids_ref[i * PER_STEP + slot] // 2))

    return pl.pallas_call(
        gather_kernel,
        out_shape=jax.ShapeDtypeStruct((entries // 4, rows, 256), BF16),
        grid_spec=pltpu.PrefetchScalarGridSpec(
            num_scalar_prefetch=1,
            grid=(entries // PER_STEP,),
            in_specs=[spec(slot) for slot in range(PER_STEP)],
            out_specs=pl.BlockSpec((PER_STEP // 4, rows, 256), lambda i, ids_ref: (i, 0, 0)),
        ),
        name="gather_blocks",
    )(ids, *([dictionary] * PER_STEP))


def share_kernel(first_ref, last_ref, split_ref, s_ref, z_ref, y_ref, out_ref, r_ref, rb_ref):
    quads = s_ref.shape[0]
    lane = lax.broadcasted_iota(jnp.int32, (PATCHES, 256), 1) // BLOCK
    r_ref[...] = -y_ref[...].astype(F32)

    def forward(quad, carry):
        z = jnp.concatenate([z_ref[2 * quad], z_ref[2 * quad + 1]], axis=1).astype(F32)
        mask = lane < split_ref[quad]
        zz = jnp.concatenate([jnp.where(mask, z, 0.0), jnp.where(mask, 0.0, z)], axis=0).astype(BF16)
        term = lax.dot_general(zz, s_ref[quad], (((1,), (1,)), ((), ())), preferred_element_type=F32)
        r_ref[first_ref[quad]] += term[:PATCHES]
        r_ref[last_ref[quad]] += term[PATCHES:]
        return carry

    lax.fori_loop(0, quads, forward, 0, unroll=4)
    rb_ref[...] = r_ref[...].astype(BF16)

    def backward(quad, carry):
        rr = jnp.concatenate([rb_ref[first_ref[quad]], rb_ref[last_ref[quad]]], axis=0)
        gr = jnp.dot(rr, s_ref[quad], preferred_element_type=F32)
        g = jnp.where(lane < split_ref[quad], gr[:PATCHES], gr[PATCHES:]).astype(BF16)
        out_ref[2 * quad] = g[:, :128]
        out_ref[2 * quad + 1] = g[:, 128:]
        return carry

    lax.fori_loop(0, quads, backward, 0, unroll=4)


def gradient_share(first, last, split, blocks, z, targets):
    groups, patches, rows = targets.shape
    smem = pl.BlockSpec(memory_space=pltpu.SMEM)
    vmem = pl.BlockSpec(memory_space=VMEM)
    return pl.pallas_call(
        share_kernel,
        out_shape=jax.ShapeDtypeStruct(z.shape, BF16),
        in_specs=[smem, smem, smem, vmem, vmem, vmem],
        out_specs=vmem,
        scratch_shapes=[VMEM((groups, patches, rows), F32), VMEM((groups, patches, rows), BF16)],
        compiler_params=pltpu.CompilerParams(vmem_limit_bytes=40 * 1024 * 1024),
        name="gradient_share",
    )(first, last, split, blocks, z, targets)


class Place:
    def __init__(self, devices):
        self.me = lax.axis_index("rows")
        self.fars = devices // 4
        self.core = self.me % 2
        self.near = (self.me // 2) % 2
        self.far = self.me // 4

    def index(self, far, near, core):
        return (far * 2 + near) * 2 + core

    def far_at(self, distance):
        return (self.far + distance) % self.fars

    def far_before(self, distance):
        return (self.far + self.fars - distance) % self.fars

    def far_peer(self, distance):
        return self.index(self.far_at(distance), self.near, self.core)

    def near_peer(self):
        return self.index(self.far, 1 - self.near, self.core)

    def core_peer(self):
        return self.index(self.far, self.near, 1 - self.core)


def send(src, dst, send_sem, recv_sem, peer):
    copy = pltpu.make_async_remote_copy(
        src_ref=src,
        dst_ref=dst,
        send_sem=send_sem,
        recv_sem=recv_sem,
        device_id=(lax.axis_index("groups"), peer),
        device_id_type=pl.DeviceIdType.MESH,
    )
    copy.start()
    return copy


def greet(at):
    barrier = pltpu.get_barrier_semaphore()
    peers = [at.core_peer(), at.near_peer()] + [at.far_peer(d) for d in range(1, at.fars)]
    for peer in peers:
        pl.semaphore_signal(
            barrier, inc=1, device_id=(lax.axis_index("groups"), peer), device_id_type=pl.DeviceIdType.MESH
        )
    pl.semaphore_wait(barrier, len(peers))


def spread(at, all_ref, sems):
    far_s, far_r, near_s, near_r, core_s, core_r = sems
    mine = all_ref.at[at.me]
    far_copies = [
        send(mine, mine, far_s.at[d - 1], far_r.at[d - 1], at.far_peer(d)) for d in range(1, at.fars)
    ]
    near_copies = [send(mine, mine, near_s.at[0], near_r.at[0], at.near_peer())]
    core_copies = [send(mine, mine, core_s.at[0], core_r.at[0], at.core_peer())]
    slot = 1
    for d in range(at.fars):
        if d:
            far_copies[d - 1].wait_recv()
            came = all_ref.at[at.index(at.far_before(d), at.near, at.core)]
            near_copies.append(send(came, came, near_s.at[d], near_r.at[d], at.near_peer()))
            core_copies.append(send(came, came, core_s.at[slot], core_r.at[slot], at.core_peer()))
            slot += 1
        if d:
            near_copies[d - 1].wait_recv()
            came = all_ref.at[at.index(at.far_before(d - 1), 1 - at.near, at.core)]
            core_copies.append(send(came, came, core_s.at[slot], core_r.at[slot], at.core_peer()))
            slot += 1
    last = at.fars - 1
    near_copies[last].wait_recv()
    came = all_ref.at[at.index(at.far_before(last), 1 - at.near, at.core)]
    core_copies.append(send(came, came, core_s.at[slot], core_r.at[slot], at.core_peer()))
    for copy in core_copies:
        copy.wait_recv()
    for copy in far_copies + near_copies + core_copies:
        copy.wait_send()


def gather_codes_kernel(devices, mine_ref, all_ref, own_sem, *sems):
    at = Place(devices)
    own = pltpu.make_async_copy(mine_ref, all_ref.at[at.me], own_sem)
    own.start()
    greet(at)
    own.wait()
    spread(at, all_ref, sems)


def spread_sems(devices):
    fars = devices // 4
    dma = pltpu.SemaphoreType.DMA
    return [dma((fars - 1,)), dma((fars - 1,)), dma((fars,)), dma((fars,)), dma((2 * fars,)), dma((2 * fars,))]


def gather_codes(devices, mine):
    vmem = pl.BlockSpec(memory_space=VMEM)
    return pl.pallas_call(
        functools.partial(gather_codes_kernel, devices),
        out_shape=jax.ShapeDtypeStruct((devices,) + mine.shape, BF16),
        in_specs=[vmem],
        out_specs=vmem,
        scratch_shapes=[pltpu.SemaphoreType.DMA] + spread_sems(devices),
        compiler_params=pltpu.CompilerParams(collective_id=0, has_side_effects=True),
        name="gather_codes",
    )(mine)


def step_kernel(
    devices, weight, share_ref, point_ref, prev_ref, thr_ref, all_ref, newpoint_ref, newprev_ref,
    got_core, got_near, got_far, sum_core, sum_near, kept,
    c_s, c_r, n_s, n_r, f_s, f_r, *sems,
):
    at = Place(devices)
    fars = at.fars
    greet(at)
    order = list(range(1, fars)) + [0]
    core_copies = {}
    for flip in (1, 0):
        for d in order:
            near = at.near if flip == 0 else 1 - at.near
            chunk = share_ref.at[at.index(at.far_at(d), near, 1 - at.core)]
            slot = flip * fars + d
            core_copies[flip, d] = send(chunk, got_core.at[slot], c_s.at[slot], c_r.at[slot], at.core_peer())
    near_copies = {}
    for d in order:
        core_copies[1, d].wait_recv()
        own = share_ref[at.index(at.far_at(d), 1 - at.near, at.core)].astype(F32)
        sum_core[d] = (own + got_core[fars + d].astype(F32)).astype(BF16)
        near_copies[d] = send(sum_core.at[d], got_near.at[d], n_s.at[d], n_r.at[d], at.near_peer())
    far_copies = {}
    for d in order:
        core_copies[0, d].wait_recv()
        own = share_ref[at.index(at.far_at(d), at.near, at.core)].astype(F32)
        total = own + got_core[d].astype(F32)
        near_copies[d].wait_recv()
        total = total + got_near[d].astype(F32)
        if d:
            sum_near[d - 1] = total.astype(BF16)
            far_copies[d] = send(sum_near.at[d - 1], got_far.at[d - 1], f_s.at[d - 1], f_r.at[d - 1], at.far_peer(d))
        else:
            kept[...] = total
    for d in range(1, fars):
        far_copies[d].wait_recv()
        kept[...] += got_far[d - 1].astype(F32)
    stepped = point_ref[...] - 0.5 * kept[...]
    thr = thr_ref[...]
    current = stepped - jnp.clip(stepped, -thr, thr)
    newprev_ref[...] = current
    point = current if weight is None else current + weight * (current - prev_ref[...])
    newpoint_ref[...] = point
    all_ref[at.me] = point.astype(BF16)
    for copy in list(core_copies.values()) + list(near_copies.values()) + list(far_copies.values()):
        copy.wait_send()
    spread(at, all_ref, sems)


def code_step(devices, turn, weight, share, point, prev, thr):
    fars = devices // 4
    chunk = point.shape
    dma = pltpu.SemaphoreType.DMA
    vmem = pl.BlockSpec(memory_space=VMEM)
    return pl.pallas_call(
        functools.partial(step_kernel, devices, weight),
        out_shape=(
            jax.ShapeDtypeStruct(share.shape, BF16),
            jax.ShapeDtypeStruct(chunk, F32),
            jax.ShapeDtypeStruct(chunk, F32),
        ),
        in_specs=[vmem] * 4,
        out_specs=(vmem, vmem, vmem),
        scratch_shapes=[
            VMEM((2 * fars,) + chunk, BF16),
            VMEM((fars,) + chunk, BF16),
            VMEM((fars - 1,) + chunk, BF16),
            VMEM((fars,) + chunk, BF16),
            VMEM((fars - 1,) + chunk, BF16),
            VMEM(chunk, F32),
            dma((2 * fars,)), dma((2 * fars,)), dma((fars,)), dma((fars,)), dma((fars - 1,)), dma((fars - 1,)),
        ]
        + spread_sems(devices),
        compiler_params=pltpu.CompilerParams(
            collective_id=1 + turn, has_side_effects=True, vmem_limit_bytes=40 * 1024 * 1024
        ),
        name="code_step%d" % turn,
    )(share, point, prev, thr)


def local(dictionary, patches, initial_codes, support, counts, group_order, penalty):
    rows = dictionary.shape[0]
    groups = group_order.shape[0]
    devices = lax.axis_size("rows")
    me = lax.axis_index("rows")
    entries = LIVE * groups
    pairs = entries // 2
    chunk_pairs = pairs // devices
    chunk_rows = chunk_pairs * PATCHES

    mine = initial_codes.reshape(SLOTS // 2, 2, PATCHES, BLOCK).transpose(0, 2, 1, 3)
    mine = mine.reshape(SLOTS // 2 * PATCHES, 2 * BLOCK)
    start_all = lax.all_gather(mine, "rows", axis=0).reshape(groups * SLOTS // 2, PATCHES, 2 * BLOCK)

    ends = jnp.cumsum(counts)
    starts = ends - counts
    entry = jnp.arange(entries, dtype=jnp.int32)
    group_of = jnp.sum((entry[:, None] >= ends[None, :]).astype(jnp.int32), axis=1)
    slot_of = entry - jnp.max(jnp.where(entry[:, None] >= starts[None, :], starts[None, :], 0), axis=1)
    ids = jnp.take(support.reshape(-1), group_of * SLOTS + slot_of)
    quads = group_of.reshape(-1, 4)
    first, last = quads[:, 0], quads[:, 3]
    split = jnp.sum((quads == first[:, None]).astype(jnp.int32), axis=1)
    seats = jnp.arange(groups, dtype=jnp.int32)[None, :]
    seat = jnp.sum(jnp.where(group_order[None, :] == group_of[:, None], seats, 0), axis=1)

    blocks = gather_blocks(dictionary, ids)
    targets = patches.T.reshape(groups, PATCHES, rows)

    source = (seat * (SLOTS // 2) + slot_of // 2).reshape(pairs, 2)
    half = (slot_of % 2).reshape(pairs, 2)[:, :, None, None] == 0

    def side(which):
        both = jnp.take(start_all, source[:, which], axis=0)
        return jnp.where(half[:, which], both[..., :BLOCK], both[..., BLOCK:])

    z_all = jnp.concatenate([side(0), side(1)], axis=2)
    thr_all = 0.5 * jnp.take(penalty, group_of, axis=0)
    own_thr = lax.dynamic_slice_in_dim(thr_all.reshape(pairs, 2, PATCHES), me * chunk_pairs, chunk_pairs, 0)
    thr = jnp.repeat(own_thr.transpose(0, 2, 1).reshape(chunk_rows, 2), BLOCK, axis=1)
    point = lax.dynamic_slice_in_dim(z_all, me * chunk_pairs, chunk_pairs, 0)
    point = point.reshape(chunk_rows, 2 * BLOCK).astype(F32)
    prev = point
    momenta = momentum_list()
    for turn in range(ITERS):
        share = gradient_share(first, last, split, blocks, z_all, targets)
        weight = momenta[turn] if turn + 1 < ITERS else None
        share = share.reshape(devices, chunk_rows, 2 * BLOCK)
        z_all, point, prev = code_step(devices, turn, weight, share, point, prev, thr)
        z_all = z_all.reshape(pairs, PATCHES, 2 * BLOCK)

    group = lax.dynamic_index_in_dim(group_order, me, 0, keepdims=False)
    begin = jnp.take(starts, group)
    live = jnp.take(counts, group)
    wanted = begin // 2 + jnp.arange(SLOTS // 2 + 1, dtype=jnp.int32)
    near = jnp.take(z_all, jnp.minimum(wanted, pairs - 1), axis=0).astype(F32)
    near = near.reshape(SLOTS // 2 + 1, PATCHES, 2, BLOCK).transpose(0, 2, 1, 3)
    near = near.reshape(SLOTS + 2, PATCHES, BLOCK)
    codes = lax.dynamic_slice_in_dim(near, begin % 2, SLOTS, 0)
    codes = jnp.where((jnp.arange(SLOTS) < live)[:, None, None], codes, 0.0)
    return codes.reshape(1, SLOTS, PATCHES * BLOCK)


def solution(mesh):
    in_specs = (
        P("rows", None),
        P("rows", "groups"),
        P(("groups", "rows"), None, None),
        P("groups", None),
        P("groups"),
        P("groups"),
        P("groups", None),
    )
    out_specs = P(("groups", "rows"), None, None)
    return jax.shard_map(local, mesh=mesh, in_specs=in_specs, out_specs=out_specs, check_vma=False)
```
